32 devices in a mesh: expert: 8 (over y, x, core), shard: 4 (over z).
Axes of the slice: x: 2, y: 2, z: 4, core: 2. Of those that a mesh axis runs over, the one named last changes fastest.
Arguments:
- block_input: float32 [64, 65, 768], P(('expert', 'shard')), may hold values from -6 to 6
- image_live: int32 [64], P(('expert', 'shard')), may hold values from 0 to 1, as said below
- expert_routes: int32 [64, 65, 2], P(('expert', 'shard')), may hold values from 0 to 7, all different within a row; in each aligned block of 130 rows (0 to 129, 130 to 259, ..., all dimensions but the last counted through in order) at most 49 rows name the same one
- first_gain: bfloat16 [768], P('shard'), may hold values from 0.5 to 1.5
- first_shift: bfloat16 [768], P('shard'), may hold values from -3 to 3
- qkv_weight: bfloat16 [768, 2304], P('shard'), may hold values from -0.21875 to 0.21875
- query_value_bias: bfloat16 [1536], P('shard'), may hold values from -2 to 2
- attn_out_weight: bfloat16 [768, 768], P('shard'), may hold values from -0.4375 to 0.4375
- attn_out_bias: bfloat16 [768], P('shard'), may hold values from -3 to 3
- second_gain: bfloat16 [768], P('shard'), may hold values from 0.5 to 1.5
- second_shift: bfloat16 [768], P('shard'), may hold values from -3 to 3
- router_weight: bfloat16 [768, 8], P('shard'), may hold values from -0.28867513 to 0.28867513
- expert_in_weight: bfloat16 [8, 768, 3072], P('expert', None, 'shard'), may hold values from -0.21875 to 0.21875
- expert_in_bias: bfloat16 [8, 3072], P('expert', 'shard'), may hold values from -3 to 3
- expert_out_weight: bfloat16 [8, 3072, 768], P('expert', None, 'shard'), may hold values from -1.75 to 1.75
- expert_out_bias: bfloat16 [8, 768], P('expert', 'shard'), may hold values from -5 to 5
- output_grad: float32 [64, 65, 768], P(('expert', 'shard')), may hold values from -6 to 6
Outputs:
- block_output: float32 [64, 65, 768], P(('expert', 'shard'))
- input_grad: float32 [64, 65, 768], P(('expert', 'shard'))
- first_gain_grad: float32 [768], P('shard')
- first_shift_grad: float32 [768], P('shard')
- qkv_weight_grad: float32 [768, 2304], P('shard')
- query_value_bias_grad: float32 [1536], P('shard')
- attn_out_weight_grad: float32 [768, 768], P('shard')
- attn_out_bias_grad: float32 [768], P('shard')
- second_gain_grad: float32 [768], P('shard')
- second_shift_grad: float32 [768], P('shard')
- router_weight_grad: float32 [768, 8], P('shard')
- expert_in_weight_grad: float32 [8, 768, 3072], P('expert', None, 'shard')
- expert_in_bias_grad: float32 [8, 3072], P('expert', 'shard')
- expert_out_weight_grad: float32 [8, 3072, 768], P('expert', None, 'shard')
- expert_out_bias_grad: float32 [8, 768], P('expert', 'shard')
The draws below stay inside these ranges and needn't reach their ends.
Inputs may be any that keep to these rules, and one draw needn't show every extreme that they name: `expert_routes`: each token names two different experts; among the rows of the image slots i with i // 2 equal, no expert is named more than 49 times, a bound that some block reaches. image_live[i] is 1 wherever i is a multiple of 2.
All inputs are finite; a program needn't handle non-finite values.
Results may differ from the reference program's by a relative error of at most 0.023.
Values may be sent and summed in bfloat16 or wider, within the bound.
A program may use at most 128 MiB of HBM per device.

```python
import math
import jax
import jax.numpy as jnp
import numpy as np
from jax import lax

D = 768
HEADS = 12
HEAD_DIM = 64
FF = 3072
SEQ = 65
IMG_DEV = 2
EXPERTS = 8
CAP = 49
IMAGES = 64


def draw_image_live(key, part):
    coin = jax.random.randint(key, (IMAGES,), 0, 4)
    first_slot = jnp.arange(IMAGES, dtype=jnp.int32) % IMG_DEV == 0
    return jnp.where(first_slot, 1, jnp.minimum(coin, 1)).astype(jnp.int32)


def draw_query_value_bias(key, part):
    noise = jnp.clip(jax.random.normal(key, (2 * D,), jnp.float32), -4.0, 4.0)
    return (noise * 0.5).astype(jnp.bfloat16)


def draw_router_weight(key, part):
    noise = jnp.clip(jax.random.normal(key, (D, EXPERTS), jnp.float32), -4.0, 4.0) * (2.0 / math.sqrt(D))
    return noise.astype(jnp.bfloat16)


def levels(key, dims, split, smallest, top_value):
    gain = 1.0
    for axis_at, parts in split:
        heights = jax.random.uniform(jax.random.fold_in(jax.random.fold_in(key, 6), axis_at), (parts,), jnp.float32, smallest / len(split), top_value / len(split))
        gain = gain * jnp.repeat(jnp.exp(heights), dims[axis_at] // parts).reshape((-1,) + (1,) * (len(dims) - 1 - axis_at))
    return gain


def deal_out(stream_key, own, number, rows, count, top, bound, slope):
    sequence = jax.random.permutation(stream_key, count)
    heavy_load, ordinary = portions_of(count, rows * top, bound, slope, True), portions_of(count, rows * top, bound, slope, False)
    places = jnp.arange(count)

    def named(tallies, rotation):
        used = int((tallies > 0).sum())
        fixed = max(1, used // 4)
        moved = fixed + (places - fixed + rotation * (used - fixed)) % max(1, count - fixed)
        return jnp.zeros((count,), jnp.int32).at[sequence[jnp.where(places < fixed, places, moved)]].set(jnp.asarray(tallies, jnp.int32))

    tallies = jnp.where(number % 4 == 0, named(heavy_load, number // 4), named(ordinary, number - number // 4 - 1))
    mixed = jax.random.permutation(jax.random.fold_in(own, 3), count)
    donor, taker = mixed[0:count // 2 * 2:2], mixed[1:count // 2 * 2:2]
    room = jnp.minimum(tallies[donor] - 1, bound - tallies[taker]) // 2
    room = jnp.where((donor == sequence[0]) | (taker == sequence[0]) | (tallies[taker] == 0), 0, jnp.maximum(room, 0))
    moved = jax.random.randint(jax.random.fold_in(own, 4), (count // 2,), 0, 1 << 20) % (room + 1)
    tallies = tallies.at[donor].add(-moved).at[taker].add(moved)
    labels = jnp.searchsorted(jnp.cumsum(tallies), jnp.arange(rows * top), side="right").astype(jnp.int32)
    grid = labels.reshape(top, rows).T
    grid = grid[jax.random.permutation(jax.random.fold_in(own, 1), rows)]
    rotation = jax.random.randint(jax.random.fold_in(own, 2), (rows, 1), 0, top)
    return jnp.take_along_axis(grid, (jnp.arange(top)[None, :] + rotation) % top, axis=1)


def portions_of(amount, total, reach, lean, full):
    loads = [(1 << 20) // math.isqrt(standing ** lean) + 1 for standing in range(1, amount + 1)]
    largest = reach if full else min(reach, max(-(-total // amount), total * loads[0] // sum(loads)))
    least = 1 if total - largest >= amount - 1 else 0
    counts, spare = [largest] + [least] * (amount - 1), total - largest - least * (amount - 1)
    while spare > 0:
        free = [i for i in range(1, amount) if counts[i] < largest] or [i for i in range(1, amount) if counts[i] < reach]
        pool, remaining = sum([loads[i] for i in free]), spare
        for i in free:
            addition = min(reach - counts[i], max(1, remaining * loads[i] // pool), spare)
            counts[i] = counts[i] + addition
            spare = spare - addition
    return np.array(counts)


def bell_draw(rng, extent, scale, most, cuts=(), kind=jnp.bfloat16):
    values = jax.random.normal(rng, extent, jnp.float32) * scale
    if len(cuts) > 0:
        values = levels(rng, extent, cuts, -0.22, 0.18) * values
    return jnp.clip(values, min=-most, max=most).astype(kind)


def setup_inputs(seed: int = 0) -> dict:
    key_of = jax.random.split(jax.random.key(seed), 18)
    block_input = bell_draw(key_of[0], (IMAGES, SEQ, D), 1.0, 6.0, ((0, 32),), jnp.float32)
    image_live = draw_image_live(jax.random.fold_in(key_of[17], 71), 0)
    expert_routes_keys = jax.random.split(jax.random.fold_in(key_of[2], 1), IMAGES * SEQ // (IMG_DEV * SEQ))
    expert_routes_turns = jax.random.permutation(jax.random.fold_in(key_of[2], 3), IMAGES * SEQ // (IMG_DEV * SEQ))
    expert_routes = jax.vmap(lambda own, number: deal_out(jax.random.fold_in(key_of[2], 2), own, number, IMG_DEV * SEQ, EXPERTS, 2, CAP, 1))(expert_routes_keys, expert_routes_turns).reshape((IMAGES, SEQ, 2))
    first_gain = jnp.clip(1.0 + 0.1 * jax.random.normal(key_of[3], (D,), jnp.float32), 0.5, 1.5).astype(jnp.bfloat16)
    first_shift = bell_draw(key_of[4], (D,), 0.5, 3.0, ((0, 4),))
    qkv_weight = bell_draw(key_of[5], (D, 3 * D), D ** -0.5, 0.21875, ((0, 4),))
    query_value_bias = draw_query_value_bias(jax.random.fold_in(key_of[17], 71), 0)
    attn_out_weight = bell_draw(key_of[7], (D, D), (D // 4) ** -0.5, 0.4375, ((0, 4),))
    attn_out_bias = bell_draw(key_of[8], (D,), 0.5, 3.0, ((0, 4),))
    second_gain = jnp.clip(1.0 + 0.1 * jax.random.normal(key_of[9], (D,), jnp.float32), 0.5, 1.5).astype(jnp.bfloat16)
    second_shift = bell_draw(key_of[10], (D,), 0.5, 3.0, ((0, 4),))
    router_weight = draw_router_weight(jax.random.fold_in(key_of[17], 71), 0)
    expert_in_weight = bell_draw(key_of[12], (EXPERTS, D, FF), D ** -0.5, 0.21875, ((0, 8), (2, 4)))
    expert_in_bias = bell_draw(key_of[13], (EXPERTS, FF), 0.5, 3.0, ((0, 8), (1, 4)))
    expert_out_weight = bell_draw(key_of[14], (EXPERTS, FF, D), (FF // 256 + 1) ** -0.5, 1.75, ((0, 8), (2, 4)))
    expert_out_bias = bell_draw(key_of[15], (EXPERTS, D), 1.0, 5.0, ((0, 8), (1, 4)))
    output_grad = bell_draw(key_of[16], (IMAGES, SEQ, D), 1.0, 6.0, ((0, 32),), jnp.float32)
    return {"block_input": block_input, "image_live": image_live, "expert_routes": expert_routes, "first_gain": first_gain, "first_shift": first_shift, "qkv_weight": qkv_weight, "query_value_bias": query_value_bias, "attn_out_weight": attn_out_weight, "attn_out_bias": attn_out_bias, "second_gain": second_gain, "second_shift": second_shift, "router_weight": router_weight, "expert_in_weight": expert_in_weight, "expert_in_bias": expert_in_bias, "expert_out_weight": expert_out_weight, "expert_out_bias": expert_out_bias, "output_grad": output_grad}


EPSILON = 1e-06
PRECISE = lax.Precision.HIGHEST
HALF_ROOT = 0.7071067811865476
DENSITY = 0.3989422804014327

def as_float(array_in):
    return array_in.astype(jnp.float32)

def contract_rows(left_side, right_side):
    return lax.dot_general(left_side, right_side, (((0,), (0,)), ((), ())), preferred_element_type=jnp.float32)

def contract_cols(left_side, right_side):
    return lax.dot_general(left_side, right_side, (((1,), (1,)), ((), ())), preferred_element_type=jnp.float32)

def precise_rows(left_side, right_side):
    return lax.dot_general(left_side, right_side, (((0,), (0,)), ((), ())), precision=PRECISE, preferred_element_type=jnp.float32)

def precise_cols(left_side, right_side):
    return lax.dot_general(left_side, right_side, (((1,), (1,)), ((), ())), precision=PRECISE, preferred_element_type=jnp.float32)

def layer_norm(values_in, gain_vec, shift_vec):
    center = values_in - lax.optimization_barrier(jnp.mean(values_in, axis=-1, keepdims=True))
    inv_std = lax.rsqrt(lax.optimization_barrier(jnp.mean(center * center, axis=-1, keepdims=True)) + EPSILON)
    normed = center * inv_std
    return (normed * as_float(gain_vec) + as_float(shift_vec), normed, inv_std)

def norm_back(upstream, normed, inv_std, gain_vec):
    scaled = upstream * as_float(gain_vec)
    return inv_std * (scaled - lax.optimization_barrier(jnp.mean(scaled, axis=-1, keepdims=True)) - normed * lax.optimization_barrier(jnp.mean(scaled * normed, axis=-1, keepdims=True)))

def gelu_parts(pre_act):
    normal_cdf = 0.5 * (1.0 + jax.scipy.special.erf(pre_act * HALF_ROOT))
    return (pre_act * normal_cdf, normal_cdf + pre_act * DENSITY * jnp.exp(-0.5 * pre_act * pre_act))

def route_tables(expert_routes, image_live, expert_count, capacity):
    row_count = expert_routes.shape[0] * expert_routes.shape[1]
    flat_routes = expert_routes.reshape(2 * row_count)
    live_rows = jnp.repeat(image_live, expert_routes.shape[1])
    alive_pairs = jnp.repeat(live_rows, 2)
    chosen = (flat_routes[:, None] == jnp.arange(expert_count, dtype=jnp.int32)[None, :]).astype(jnp.int32)
    live_hits = chosen * alive_pairs[:, None]
    position = lax.optimization_barrier(jnp.sum((jnp.cumsum(live_hits, axis=0, dtype=jnp.int32) - live_hits) * live_hits, axis=1, dtype=jnp.int32))
    slot_index = flat_routes * capacity + position
    slot_table = ((slot_index[None, :] == jnp.arange(expert_count * capacity, dtype=jnp.int32)[:, None]) & (alive_pairs[None, :] > 0)).astype(jnp.bfloat16)
    return (chosen.reshape(row_count, 2, expert_count), slot_table, live_rows)

def attention_scores(query_rows, key_rows):
    return jnp.einsum('bqhd,bkhd->bhqk', as_float(query_rows), as_float(key_rows)) * (1.0 / math.sqrt(HEAD_DIM))

def forward_device(tokens, image_live, expert_routes, output_grad, params):
    first_gain, first_shift, qkv_weight, query_value_bias, attn_out_weight, attn_out_bias, second_gain, second_shift, router_weight = params
    row_count = IMG_DEV * SEQ
    flat_tokens = tokens.reshape(row_count, D)
    norm_out, normed_one, inv_one = layer_norm(flat_tokens, first_gain, first_shift)
    attn_in = norm_out.astype(jnp.bfloat16)
    bias_row = jnp.concatenate([as_float(query_value_bias[:D]), jnp.zeros((D,), jnp.float32), as_float(query_value_bias[D:])])
    packed = (jnp.dot(attn_in, qkv_weight, preferred_element_type=jnp.float32) + bias_row).astype(jnp.bfloat16).reshape(IMG_DEV, SEQ, 3, HEADS, HEAD_DIM)
    query_rows = packed[:, :, 0]
    key_rows = packed[:, :, 1]
    value_rows = packed[:, :, 2]
    scores = attention_scores(query_rows, key_rows)
    row_max = lax.optimization_barrier(jnp.max(scores, axis=-1, keepdims=True))
    log_total = row_max + jnp.log(lax.optimization_barrier(jnp.sum(jnp.exp(scores - row_max), axis=-1, keepdims=True)))
    weights = jnp.exp(scores - log_total).astype(jnp.bfloat16)
    mixed_heads = jnp.einsum('bhqk,bkhd->bqhd', as_float(weights), as_float(value_rows)).astype(jnp.bfloat16).reshape(row_count, D)
    residual = flat_tokens + jnp.dot(mixed_heads, attn_out_weight, preferred_element_type=jnp.float32) + as_float(attn_out_bias)
    norm_two_out, normed_two, inv_two = layer_norm(residual, second_gain, second_shift)
    expert_in = norm_two_out.astype(jnp.bfloat16)
    logits = jnp.dot(expert_in, router_weight, preferred_element_type=jnp.float32)
    shifted = jnp.exp(logits - lax.optimization_barrier(jnp.max(logits, axis=-1, keepdims=True)))
    gate_probs = shifted / lax.optimization_barrier(jnp.sum(shifted, axis=-1, keepdims=True))
    chosen, slot_table, live_rows = route_tables(expert_routes, image_live, EXPERTS, CAP)
    gate_pick = lax.optimization_barrier(jnp.sum(gate_probs[:, None, :] * as_float(chosen), axis=2))
    upstream = output_grad.reshape(row_count, D) * as_float(live_rows)[:, None]
    send_table = lax.optimization_barrier(jnp.sum(slot_table.reshape(EXPERTS * CAP, row_count, 2), axis=2))
    outgoing = jnp.dot(send_table, expert_in, preferred_element_type=jnp.float32).astype(jnp.bfloat16)
    sent_grad = (gate_pick[:, :, None] * upstream[:, None, :]).astype(jnp.bfloat16).reshape(2 * row_count, D)
    grad_out = jnp.dot(slot_table, sent_grad, preferred_element_type=jnp.float32).astype(jnp.bfloat16)
    kept = (normed_one, inv_one, attn_in, query_rows, key_rows, value_rows, log_total, mixed_heads, residual, normed_two, inv_two, expert_in, gate_probs, chosen, slot_table, gate_pick, upstream, live_rows)
    return (outgoing, grad_out, kept)

def expert_pass(inputs):
    rows_in, grads_in, in_weight, in_bias, out_weight, out_bias = inputs
    pre_act = jnp.dot(rows_in, in_weight, preferred_element_type=jnp.float32) + as_float(in_bias)
    gelu_out, gelu_slope = gelu_parts(pre_act)
    gelu_bf = gelu_out.astype(jnp.bfloat16)
    expert_out = (jnp.dot(gelu_bf, out_weight, preferred_element_type=jnp.float32) + as_float(out_bias)).astype(jnp.bfloat16)
    out_bias_grad = lax.optimization_barrier(jnp.sum(as_float(grads_in), axis=0))
    out_weight_grad = contract_rows(gelu_bf, grads_in)
    pre_grad = contract_cols(grads_in, out_weight) * gelu_slope
    in_bias_grad = lax.optimization_barrier(jnp.sum(pre_grad, axis=0))
    pre_bf = pre_grad.astype(jnp.bfloat16)
    in_weight_grad = contract_rows(rows_in, pre_bf)
    back_rows = contract_cols(pre_bf, in_weight).astype(jnp.bfloat16)
    return (expert_out, back_rows, in_weight_grad, in_bias_grad, out_weight_grad, out_bias_grad)

def backward_device(returned, returned_grad, kept, params):
    first_gain, first_shift, qkv_weight, query_value_bias, attn_out_weight, attn_out_bias, second_gain, second_shift, router_weight = params
    normed_one, inv_one, attn_in, query_rows, key_rows, value_rows, log_total, mixed_heads, residual, normed_two, inv_two, expert_in, gate_probs, chosen, slot_table, gate_pick, upstream, live_rows = kept
    row_count = IMG_DEV * SEQ
    picked = contract_rows(slot_table, returned).reshape(row_count, 2, D)
    live_col = as_float(live_rows)[:, None]
    block_output = residual + live_col * lax.optimization_barrier(jnp.sum(gate_pick[:, :, None] * picked, axis=1))
    gate_grad = lax.optimization_barrier(jnp.sum(upstream[:, None, :] * picked, axis=2))
    full_gate_grad = lax.optimization_barrier(jnp.sum(gate_grad[:, :, None] * as_float(chosen), axis=1))
    logit_grad = gate_probs * (full_gate_grad - lax.optimization_barrier(jnp.sum(gate_probs * full_gate_grad, axis=-1, keepdims=True)))
    router_grad = precise_rows(as_float(expert_in), logit_grad)
    route_grad = lax.optimization_barrier(jnp.sum(contract_rows(slot_table, returned_grad).reshape(row_count, 2, D), axis=1))
    normed_two_grad = route_grad + precise_cols(logit_grad, as_float(router_weight))
    second_gain_grad = lax.optimization_barrier(jnp.sum(normed_two_grad * normed_two, axis=0))
    second_shift_grad = lax.optimization_barrier(jnp.sum(normed_two_grad, axis=0))
    residual_grad = upstream + norm_back(normed_two_grad, normed_two, inv_two, second_gain)
    proj_bias_grad = lax.optimization_barrier(jnp.sum(residual_grad, axis=0))
    residual_bf = residual_grad.astype(jnp.bfloat16)
    proj_grad = contract_rows(mixed_heads, residual_bf)
    mixed_grad = contract_cols(residual_bf, attn_out_weight).astype(jnp.bfloat16).reshape(IMG_DEV, SEQ, HEADS, HEAD_DIM)
    scores = attention_scores(query_rows, key_rows)
    probs = jnp.exp(scores - log_total)
    probs_bf = probs.astype(jnp.bfloat16)
    value_grad = jnp.einsum('bhqk,bqhd->bkhd', as_float(probs_bf), as_float(mixed_grad))
    prob_grad = jnp.einsum('bqhd,bkhd->bhqk', as_float(mixed_grad), as_float(value_rows))
    score_grad = (probs * (prob_grad - lax.optimization_barrier(jnp.sum(probs * prob_grad, axis=-1, keepdims=True))) * (1.0 / math.sqrt(HEAD_DIM))).astype(jnp.bfloat16)
    query_grad = jnp.einsum('bhqk,bkhd->bqhd', as_float(score_grad), as_float(key_rows))
    key_grad = jnp.einsum('bhqk,bqhd->bkhd', as_float(score_grad), as_float(query_rows))
    bias_grad = jnp.concatenate([lax.optimization_barrier(jnp.sum(query_grad.reshape(row_count, D), axis=0)), lax.optimization_barrier(jnp.sum(value_grad.reshape(row_count, D), axis=0))])
    packed_grad = jnp.stack([query_grad, key_grad, value_grad], axis=2).reshape(row_count, 3 * D).astype(jnp.bfloat16)
    qkv_grad = contract_rows(attn_in, packed_grad)
    normed_one_grad = contract_cols(packed_grad, qkv_weight)
    first_gain_grad = lax.optimization_barrier(jnp.sum(normed_one_grad * normed_one, axis=0))
    first_shift_grad = lax.optimization_barrier(jnp.sum(normed_one_grad, axis=0))
    input_grad = residual_grad + norm_back(normed_one_grad, normed_one, inv_one, first_gain)
    grads = (first_gain_grad, first_shift_grad, qkv_grad, bias_grad, proj_grad, proj_bias_grad, second_gain_grad, second_shift_grad, router_grad)
    return ((block_output.reshape(IMG_DEV, SEQ, D), input_grad.reshape(IMG_DEV, SEQ, D)), grads)

def reference(block_input, image_live, expert_routes, first_gain, first_shift, qkv_weight, query_value_bias, attn_out_weight, attn_out_bias, second_gain, second_shift, router_weight, expert_in_weight, expert_in_bias, expert_out_weight, expert_out_bias, output_grad):
    device_count = IMAGES // IMG_DEV
    params = (first_gain, first_shift, qkv_weight, query_value_bias, attn_out_weight, attn_out_bias, second_gain, second_shift, router_weight)

    def front(inputs):
        return forward_device(inputs[0], inputs[1], inputs[2], inputs[3], params)
    outgoing, grad_out, kept = lax.map(front, (block_input.reshape(device_count, IMG_DEV, SEQ, D), image_live.reshape(device_count, IMG_DEV), expert_routes.reshape(device_count, IMG_DEV, SEQ, 2), output_grad.reshape(device_count, IMG_DEV, SEQ, D)))

    def regroup(stacked):
        return stacked.reshape(device_count, EXPERTS, CAP, D).transpose(1, 0, 2, 3).reshape(EXPERTS, device_count * CAP, D)

    def ungroup(stacked):
        return stacked.reshape(EXPERTS, device_count, CAP, D).transpose(1, 0, 2, 3).reshape(device_count, EXPERTS * CAP, D)
    expert_out, back_rows, in_weight_grad, in_bias_grad, out_weight_grad, out_bias_grad = lax.map(expert_pass, (regroup(outgoing), regroup(grad_out), expert_in_weight, expert_in_bias, expert_out_weight, expert_out_bias))

    def back_step(running, inputs):
        outputs, grads = backward_device(inputs[0], inputs[1], inputs[2], params)
        return (jax.tree.map(jnp.add, running, grads), outputs)
    zero_grads = tuple((jnp.zeros(param.shape, jnp.float32) for param in params))
    sums, outputs = lax.scan(back_step, zero_grads, (ungroup(expert_out), ungroup(back_rows), kept))
    block_output = outputs[0].reshape(IMAGES, SEQ, D)
    input_grad = outputs[1].reshape(IMAGES, SEQ, D)
    return (block_output, input_grad, sums[0], sums[1], sums[2], sums[3], sums[4], sums[5], sums[6], sums[7], sums[8], in_weight_grad, in_bias_grad, out_weight_grad, out_bias_grad)
```

```python
import math

import jax
import jax.numpy as jnp
from jax import lax
from jax.sharding import PartitionSpec as P

HEADS = 12
HEAD_DIM = 64


EPSILON = 1e-06
PRECISE = lax.Precision.HIGHEST
HALF_ROOT = 0.7071067811865476
DENSITY = 0.3989422804014327


def as_float(array_in):
    return array_in.astype(jnp.float32)


def contract_rows(left_side, right_side):
    return lax.dot_general(
        left_side, right_side, (((0,), (0,)), ((), ())), preferred_element_type=jnp.float32
    )


def contract_cols(left_side, right_side):
    return lax.dot_general(
        left_side, right_side, (((1,), (1,)), ((), ())), preferred_element_type=jnp.float32
    )


def precise_rows(left_side, right_side):
    return lax.dot_general(
        left_side,
        right_side,
        (((0,), (0,)), ((), ())),
        precision=PRECISE,
        preferred_element_type=jnp.float32,
    )


def precise_cols(left_side, right_side):
    return lax.dot_general(
        left_side,
        right_side,
        (((1,), (1,)), ((), ())),
        precision=PRECISE,
        preferred_element_type=jnp.float32,
    )


def layer_norm(values_in, gain_vec, shift_vec):
    center = values_in - jnp.mean(values_in, axis=-1, keepdims=True)
    inv_std = lax.rsqrt(jnp.mean(center * center, axis=-1, keepdims=True) + EPSILON)
    normed = center * inv_std
    return (normed * as_float(gain_vec) + as_float(shift_vec), normed, inv_std)


def norm_back(upstream, normed, inv_std, gain_vec):
    scaled = upstream * as_float(gain_vec)
    return inv_std * (
        scaled
        - jnp.mean(scaled, axis=-1, keepdims=True)
        - normed * jnp.mean(scaled * normed, axis=-1, keepdims=True)
    )


def gelu_parts(pre_act):
    normal_cdf = 0.5 * (1.0 + jax.scipy.special.erf(pre_act * HALF_ROOT))
    return (
        pre_act * normal_cdf,
        normal_cdf + pre_act * DENSITY * jnp.exp(-0.5 * pre_act * pre_act),
    )


def slot_places(expert_routes, image_live, expert_count):
    row_count = expert_routes.shape[0] * expert_routes.shape[1]
    flat_routes = expert_routes.reshape(2 * row_count)
    live_rows = jnp.repeat(image_live, expert_routes.shape[1])
    alive_pairs = jnp.repeat(live_rows, 2)
    chosen = (flat_routes[:, None] == jnp.arange(expert_count, dtype=jnp.int32)[None, :]).astype(
        jnp.int32
    )
    live_hits = chosen * alive_pairs[:, None]
    earlier = (
        jnp.arange(2 * row_count, dtype=jnp.int32)[:, None]
        > jnp.arange(2 * row_count, dtype=jnp.int32)[None, :]
    ).astype(jnp.bfloat16)
    counted = jnp.dot(earlier, live_hits.astype(jnp.bfloat16), preferred_element_type=jnp.float32)
    position = jnp.sum(counted * as_float(live_hits), axis=1)
    route_code = jnp.where(alive_pairs > 0, flat_routes, -1).astype(jnp.float32)
    return (
        chosen.reshape(row_count, 2, expert_count),
        route_code.reshape(row_count, 2),
        position.reshape(row_count, 2),
        live_rows,
    )


def attention_scores(query_rows, key_rows):
    return jnp.einsum(
        "bqhd,bkhd->bhqk", query_rows, key_rows, preferred_element_type=jnp.float32
    ) * (1.0 / math.sqrt(HEAD_DIM))


def gather_all(piece):
    return lax.all_gather(piece, ("shard", "expert"), axis=0, tiled=True)


def body(
    block_input,
    image_live,
    expert_routes,
    first_gain,
    first_shift,
    qkv_weight,
    query_value_bias,
    attn_out_weight,
    attn_out_bias,
    second_gain,
    second_shift,
    router_weight,
    expert_in_weight,
    expert_in_bias,
    expert_out_weight,
    expert_out_bias,
    output_grad,
):
    image_count, seq_length, width = block_input.shape
    row_count = image_count * seq_length
    shards = lax.axis_size("shard")
    experts = lax.axis_size("expert")
    expert_count = router_weight.shape[1]
    my_shard = lax.axis_index("shard")
    my_expert = lax.axis_index("expert")
    shard_rows = first_gain.shape[0]
    piece_rows = shard_rows // experts
    capacity = (3 * row_count + expert_count - 1) // expert_count
    group_rows = -(-shards * capacity // 16) * 16
    slot_rows = expert_count * group_rows
    sent_rows = -(-row_count // 16) * 16
    spare_rows = sent_rows - row_count
    bf16 = jnp.bfloat16

    vectors = jnp.stack(
        [
            first_gain,
            first_shift,
            attn_out_bias,
            second_gain,
            second_shift,
            query_value_bias[:shard_rows],
            query_value_bias[shard_rows:],
        ],
        axis=1,
    )
    extra = jnp.concatenate([vectors, router_weight], axis=1)
    vector_count = vectors.shape[1]
    extra = jnp.pad(extra, ((0, 0), (0, 128 - extra.shape[1])))
    packed_params = jnp.concatenate([qkv_weight, extra], axis=1)
    piece = lax.dynamic_slice_in_dim(packed_params, my_expert * piece_rows, piece_rows, axis=0)
    proj_piece = lax.dynamic_slice_in_dim(
        attn_out_weight, my_expert * piece_rows, piece_rows, axis=0
    )
    whole = gather_all(piece)
    proj_piece, whole = lax.optimization_barrier((proj_piece, whole))
    proj_full = gather_all(proj_piece)
    qkv_full = whole[:, : 3 * width]
    extra_t = as_float(whole[:, 3 * width :].T)
    gain_one, shift_one, proj_bias, gain_two, shift_two = (extra_t[i] for i in range(5))
    bias_full = jnp.stack(
        [extra_t[5].reshape(shards, shard_rows), extra_t[6].reshape(shards, shard_rows)], axis=1
    ).reshape(2 * width)
    router_t = extra_t[vector_count : vector_count + expert_count].astype(bf16)

    out_slice = lax.all_to_all(
        expert_out_weight[0], "shard", split_axis=0, concat_axis=1, tiled=True
    )
    in_slice = expert_in_weight[0]

    chosen, route_code, position, live_rows = slot_places(expert_routes, image_live, expert_count)
    live_col = as_float(live_rows)[:, None]
    upstream = output_grad.reshape(row_count, width) * live_col
    sent_up = jnp.pad(upstream.astype(bf16), ((0, spare_rows), (0, 0)))
    sent_up, proj_full = lax.optimization_barrier((sent_up, proj_full))
    line_up = lax.all_gather(sent_up, "shard", axis=0, tiled=True)

    flat_tokens = block_input.reshape(row_count, width)
    norm_out, normed_one, inv_one = layer_norm(flat_tokens, gain_one, shift_one)
    attn_in = norm_out.astype(bf16)
    bias_row = jnp.concatenate(
        [bias_full[:width], jnp.zeros((width,), jnp.float32), bias_full[width:]]
    )
    packed = (
        (jnp.dot(attn_in, qkv_full, preferred_element_type=jnp.float32) + bias_row)
        .astype(bf16)
        .reshape(image_count, seq_length, 3, HEADS, HEAD_DIM)
    )
    query_rows = packed[:, :, 0]
    key_rows = packed[:, :, 1]
    value_rows = packed[:, :, 2]
    scores = attention_scores(query_rows, key_rows)
    row_max = jnp.max(scores, axis=-1, keepdims=True)
    log_total = row_max + jnp.log(jnp.sum(jnp.exp(scores - row_max), axis=-1, keepdims=True))
    probs = jnp.exp(scores - log_total)
    weights = probs.astype(bf16)
    mixed_heads = (
        jnp.einsum("bhqk,bkhd->bqhd", weights, value_rows, preferred_element_type=jnp.float32)
        .astype(bf16)
        .reshape(row_count, width)
    )
    residual = (
        flat_tokens
        + jnp.dot(mixed_heads, proj_full, preferred_element_type=jnp.float32)
        + proj_bias
    )
    norm_two_out, normed_two, inv_two = layer_norm(residual, gain_two, shift_two)
    expert_in = norm_two_out.astype(bf16)
    logits = contract_cols(expert_in, router_t)
    shifted = jnp.exp(logits - jnp.max(logits, axis=-1, keepdims=True))
    gate_probs = shifted / jnp.sum(shifted, axis=-1, keepdims=True)
    gate_pick = jnp.sum(gate_probs[:, None, :] * as_float(chosen), axis=2)

    gate_high = gate_pick.astype(bf16)
    gate_low = (gate_pick - as_float(gate_high)).astype(bf16)
    notes = jnp.concatenate(
        [gate_high, gate_low, route_code.astype(bf16), position.astype(bf16)], axis=1
    )
    notes = jnp.pad(notes, ((0, 0), (0, 128 - notes.shape[1])))
    sent_line = jnp.concatenate([expert_in, notes], axis=1)
    sent_line = jnp.pad(sent_line, ((0, spare_rows), (0, 0)))
    line = lax.all_gather(sent_line, "shard", axis=0, tiled=True)
    line_rows = shards * sent_rows
    line_in = line[:, :width]
    line_notes = as_float(line[:, width : width + 8])
    line_gate = line_notes[:, 0:2] + line_notes[:, 2:4]
    line_ids = jnp.arange(line_rows, dtype=jnp.int32)[:, None]
    owner = line_ids // sent_rows
    filled = line_ids % sent_rows < row_count
    line_slot = (
        line_notes[:, 4:6].astype(jnp.int32) * group_rows
        + owner * capacity
        + line_notes[:, 6:8].astype(jnp.int32)
    )
    line_slot = jnp.where(filled & (line_notes[:, 4:6] >= 0), line_slot, -1)
    slot_ids = jnp.arange(slot_rows, dtype=jnp.int32)
    table_0 = line_slot[:, 0:1] == slot_ids[None, :]
    table_1 = line_slot[:, 1:2] == slot_ids[None, :]
    send_table = (table_0 | table_1).astype(bf16)
    grad_table = (
        jnp.where(table_0, line_gate[:, 0:1], 0.0) + jnp.where(table_1, line_gate[:, 1:2], 0.0)
    ).astype(bf16)
    outgoing = contract_rows(send_table, line_in).astype(bf16)
    incoming = lax.all_to_all(outgoing, "expert", split_axis=0, concat_axis=0, tiled=True)
    grad_out = contract_rows(grad_table, line_up).astype(bf16)
    grad_in = lax.all_to_all(grad_out, "expert", split_axis=0, concat_axis=0, tiled=True)

    pre_act = jnp.dot(incoming, in_slice, preferred_element_type=jnp.float32) + as_float(
        expert_in_bias
    )
    gelu_out, gelu_slope = gelu_parts(pre_act)
    gelu_bf = gelu_out.astype(bf16)
    own_bias = lax.dynamic_update_slice(
        jnp.zeros((1, width), jnp.float32),
        as_float(expert_out_bias),
        (0, my_shard * shard_rows),
    )
    expert_out = (
        jnp.dot(gelu_bf, out_slice, preferred_element_type=jnp.float32) + own_bias
    ).astype(bf16)
    returned = lax.all_to_all(expert_out, "expert", split_axis=0, concat_axis=0, tiled=True)
    pre_grad = contract_cols(grad_in, out_slice) * gelu_slope
    in_bias_part = jnp.sum(pre_grad, axis=0)[None]
    pre_bf = pre_grad.astype(bf16)
    back_rows = contract_cols(pre_bf, in_slice).astype(bf16)
    returned_grad = lax.all_to_all(back_rows, "expert", split_axis=0, concat_axis=0, tiled=True)
    out_weight_grad = contract_rows(gelu_bf, grad_in).astype(bf16)
    out_weight_part = as_float(
        lax.all_to_all(out_weight_grad, "shard", split_axis=1, concat_axis=0, tiled=True)
    )[None]
    in_weight_part = contract_rows(incoming, pre_bf)[None]
    out_bias_part = lax.dynamic_slice_in_dim(
        jnp.sum(as_float(grad_in), axis=0), my_shard * shard_rows, shard_rows
    )[None]

    out_0 = jnp.dot(table_0.astype(bf16), returned, preferred_element_type=jnp.float32)
    out_1 = jnp.dot(table_1.astype(bf16), returned, preferred_element_type=jnp.float32)
    combined = line_gate[:, 0:1] * out_0 + line_gate[:, 1:2] * out_1
    line_up_wide = as_float(line_up)
    gate_grad_line = jnp.stack(
        [jnp.sum(line_up_wide * out_0, axis=1), jnp.sum(line_up_wide * out_1, axis=1)], axis=1
    )
    summed = as_float(
        lax.psum_scatter(
            jnp.concatenate(
                [
                    combined.astype(bf16),
                    jnp.pad(gate_grad_line, ((0, 0), (0, 126))).astype(bf16),
                ],
                axis=1,
            ),
            "shard",
            scatter_dimension=0,
            tiled=True,
        )
    )[:row_count]
    block_output = residual + summed[:, :width]
    gate_grad = summed[:, width : width + 2]
    back_line = jnp.dot(send_table, returned_grad, preferred_element_type=jnp.float32)
    route_grad = as_float(
        lax.psum_scatter(back_line.astype(bf16), "shard", scatter_dimension=0, tiled=True)
    )[:row_count]

    full_gate_grad = jnp.sum(gate_grad[:, :, None] * as_float(chosen), axis=1)
    logit_grad = gate_probs * (
        full_gate_grad - jnp.sum(gate_probs * full_gate_grad, axis=-1, keepdims=True)
    )
    router_grad_t = contract_rows(logit_grad, as_float(expert_in))
    normed_two_grad = route_grad + jnp.dot(
        logit_grad, as_float(router_t), preferred_element_type=jnp.float32
    )
    second_gain_grad = jnp.sum(normed_two_grad * normed_two, axis=0)
    second_shift_grad = jnp.sum(normed_two_grad, axis=0)
    residual_grad = upstream + norm_back(normed_two_grad, normed_two, inv_two, gain_two)
    proj_bias_grad = jnp.sum(residual_grad, axis=0)
    residual_bf = residual_grad.astype(bf16)
    proj_grad = contract_rows(mixed_heads, residual_bf)
    mixed_grad = (
        contract_cols(residual_bf, proj_full)
        .astype(bf16)
        .reshape(image_count, seq_length, HEADS, HEAD_DIM)
    )
    value_grad = jnp.einsum(
        "bhqk,bqhd->bkhd", weights, mixed_grad, preferred_element_type=jnp.float32
    )
    prob_grad = jnp.einsum(
        "bqhd,bkhd->bhqk", mixed_grad, value_rows, preferred_element_type=jnp.float32
    )
    score_grad = (
        probs
        * (prob_grad - jnp.sum(probs * prob_grad, axis=-1, keepdims=True))
        * (1.0 / math.sqrt(HEAD_DIM))
    ).astype(bf16)
    query_grad = jnp.einsum(
        "bhqk,bkhd->bqhd", score_grad, key_rows, preferred_element_type=jnp.float32
    )
    key_grad = jnp.einsum(
        "bhqk,bqhd->bkhd", score_grad, query_rows, preferred_element_type=jnp.float32
    )
    query_bias_grad = jnp.sum(query_grad.reshape(row_count, width), axis=0)
    value_bias_grad = jnp.sum(value_grad.reshape(row_count, width), axis=0)
    packed_grad = (
        jnp.stack([query_grad, key_grad, value_grad], axis=2)
        .reshape(row_count, 3 * width)
        .astype(bf16)
    )
    qkv_grad = contract_rows(attn_in, packed_grad)
    normed_one_grad = contract_cols(packed_grad, qkv_full)
    first_gain_grad = jnp.sum(normed_one_grad * normed_one, axis=0)
    first_shift_grad = jnp.sum(normed_one_grad, axis=0)
    input_grad = residual_grad + norm_back(normed_one_grad, normed_one, inv_one, gain_one)

    bias_grad = jnp.concatenate([query_bias_grad, value_bias_grad]).reshape(shards, 2, shard_rows)
    extra_grad = jnp.concatenate(
        [
            jnp.stack(
                [
                    first_gain_grad,
                    first_shift_grad,
                    proj_bias_grad,
                    second_gain_grad,
                    second_shift_grad,
                    bias_grad[:, 0].reshape(width),
                    bias_grad[:, 1].reshape(width),
                ]
            ),
            router_grad_t,
        ],
        axis=0,
    )
    extra_grad = jnp.pad(extra_grad, ((0, 128 - extra_grad.shape[0]), (0, 0)))
    grads = jnp.concatenate(
        [qkv_grad.astype(bf16), proj_grad.astype(bf16), extra_grad.astype(bf16).T], axis=1
    )
    mine = lax.psum_scatter(grads, ("shard", "expert"), scatter_dimension=0, tiled=True)
    sums = as_float(lax.all_gather(mine, "expert", axis=0, tiled=True))
    side_t = sums[:, 4 * width :].T
    return (
        block_output.reshape(image_count, seq_length, width),
        input_grad.reshape(image_count, seq_length, width),
        side_t[0],
        side_t[1],
        sums[:, : 3 * width],
        side_t[5:7].reshape(2 * shard_rows),
        sums[:, 3 * width : 4 * width],
        side_t[2],
        side_t[3],
        side_t[4],
        sums[:, 4 * width + vector_count : 4 * width + vector_count + expert_count],
        in_weight_part,
        in_bias_part,
        out_weight_part,
        out_bias_part,
    )


def solution(mesh):
    in_specs = (
        P(("expert", "shard"), None, None),
        P(("expert", "shard")),
        P(("expert", "shard"), None, None),
        P("shard"),
        P("shard"),
        P("shard", None),
        P("shard"),
        P("shard", None),
        P("shard"),
        P("shard"),
        P("shard"),
        P("shard", None),
        P("expert", None, "shard"),
        P("expert", "shard"),
        P("expert", None, "shard"),
        P("expert", "shard"),
        P(("expert", "shard"), None, None),
    )
    out_specs = (
        P(("expert", "shard"), None, None),
        P(("expert", "shard"), None, None),
        P("shard"),
        P("shard"),
        P("shard", None),
        P("shard"),
        P("shard", None),
        P("shard"),
        P("shard"),
        P("shard"),
        P("shard", None),
        P("expert", None, "shard"),
        P("expert", "shard"),
        P("expert", None, "shard"),
        P("expert", "shard"),
    )
    return jax.shard_map(body, mesh=mesh, in_specs=in_specs, out_specs=out_specs, check_vma=False)
```
